512 devices in a mesh: traj: 64 (over x, z_lo, core), lat: 8 (over z_hi, y).
Axes of the slice: x: 4, y: 4, z: 16 (z_hi: 2, z_lo: 8; z = z_hi * 8 + z_lo), core: 2. Of those that a mesh axis runs over, the one named last changes fastest.
Arguments:
- ensemble: float32 [64, 56, 192, 384], P('traj', None, 'lat'), may hold values from -4 to 4
- counts: int32 [64], P('traj'), may hold values from 0 to 4, as said below
- mixing: bfloat16 [56, 56], replicated, may hold values from -0.75 to 0.75
- weights: float32 [192], P('lat'), may hold values from 0.5 to 1.5
- legendre: bfloat16 [128, 192, 128], P('lat'), may hold values from -0.5 to 0.5
- to_modes: float32 [56, 56], replicated, may hold values from -0.75 to 0.75
- from_modes: float32 [56, 56], replicated, may hold values from -0.75 to 0.75
- mode_rates: float32 [56], replicated, may hold values from 0.1 to 10
Outputs:
- advanced: float32 [64, 56, 192, 384], P('traj', None, 'lat')
The draws below stay inside these ranges and needn't reach their ends.
Inputs may be any that keep to these rules, and one draw needn't show every extreme that they name: The counts of all members sum to 64, and some member has exactly 4.
All inputs are finite; a program needn't handle non-finite values.
Results may differ from the reference program's by a relative error of at most 0.015.
Values may be sent and summed in bfloat16 or wider, within the bound.
No kernel may reach another device: no remote copies, remote signals or barrier semaphores. Data moves between devices by JAX's collectives and lax.ppermute only.
A program may use at most 64 MiB of HBM per device.

```python
import math
import jax
import jax.numpy as jnp
from jax import lax

NLON = 384
NLAT = 192
M = 128
NTOT = 128
LEV = 56
MEMBERS = 64


def draw_counts(key, part):
    key_one, key_two, key_three = jax.random.split(jax.random.fold_in(key, 7), 3)
    upper = MEMBERS // 8 + 1
    fours = jax.random.randint(key_one, (), 1, upper).astype(jnp.int32)
    twos = jax.random.randint(key_two, (), 1, upper).astype(jnp.int32)
    singles = MEMBERS - 4 * fours - 2 * twos
    shuffle = jax.random.permutation(key_three, MEMBERS).astype(jnp.int32)
    ranks = jnp.zeros((MEMBERS,), jnp.int32).at[shuffle].set(jnp.arange(MEMBERS, dtype=jnp.int32))
    result = jnp.where(ranks < fours, 4, jnp.where(ranks < fours + twos, 2, jnp.where(ranks < fours + twos + singles, 1, 0)))
    return result.astype(jnp.int32)


def shard_levels(rng, shape, cuts, low, top_value):
    factor_of, own = 1.0, jax.random.fold_in(rng, 6)
    for axis_at, blocks in cuts:
        heights = jnp.exp(jax.random.uniform(jax.random.fold_in(own, axis_at), (blocks,), jnp.float32, low / len(cuts), top_value / len(cuts)))
        factor_of = factor_of * jnp.repeat(heights, shape[axis_at] // blocks).reshape([-1 if axis == axis_at else 1 for axis in range(len(shape))])
    return factor_of


def centred(stream_key, dims, width, bound, cuts=(), kind=jnp.bfloat16):
    loudness = shard_levels(stream_key, dims, cuts, -0.22, 0.18) if cuts else 1.0
    drawn = jax.random.normal(stream_key, dims, jnp.float32) * width * loudness
    return jnp.minimum(jnp.maximum(drawn, -bound), bound).astype(kind)


def setup_inputs(seed: int = 0) -> dict:
    key_of = jax.random.split(jax.random.key(seed), 9)
    return {
        "ensemble": centred(key_of[0], (MEMBERS, LEV, NLAT, NLON), 1.0, 4.0, ((0, 64), (2, 8)), jnp.float32),
        "counts": draw_counts(jax.random.fold_in(key_of[8], 71), 0),
        "mixing": centred(key_of[2], (LEV, LEV), LEV ** -0.5, 0.75),
        "weights": jnp.clip(0.5 + 1.0 * jax.random.uniform(key_of[3], (NLAT,), jnp.float32) ** shard_levels(key_of[3], (NLAT,), ((0, 8),), -0.2, 0.2), 0.5, 1.5),
        "legendre": centred(key_of[4], (M, NLAT, NTOT), ((NLAT + NTOT) // 2) ** -0.5, 0.5, ((0, 8),)),
        "to_modes": centred(key_of[5], (LEV, LEV), LEV ** -0.5, 0.75, (), jnp.float32),
        "from_modes": centred(key_of[6], (LEV, LEV), LEV ** -0.5, 0.75, (), jnp.float32),
        "mode_rates": jnp.clip(jnp.exp(jax.random.uniform(key_of[7], (LEV,), jnp.float32, math.log(0.1), math.log(10.0))), 0.1, 10.0),
    }


time_step = 0.3
cubic_rate = 0.1


def clone_sources(counts):
    living = (counts > 0).astype(jnp.int32)
    surplus_end = jnp.cumsum(jnp.maximum(counts - 1, 0), dtype=jnp.int32)
    killed_rank = jnp.cumsum(1 - living, dtype=jnp.int32) - (1 - living)
    pulled = jnp.sum((surplus_end[None, :] <= killed_rank[:, None]).astype(jnp.int32), axis=1, dtype=jnp.int32)
    members = jnp.arange(counts.shape[0], dtype=jnp.int32)
    return jnp.where(living > 0, members, pulled).astype(jnp.int32)


def fourier_tables(wavenumber, component, longitudes):
    positions = jnp.arange(longitudes, dtype=jnp.int32)
    product_index = (positions[:, None] * wavenumber[None, :]) % longitudes
    angles = (2.0 * math.pi / longitudes) * product_index.astype(jnp.float32)
    signed = jnp.where(component[None, :] == 0, jnp.cos(angles), -jnp.sin(angles))
    factor = jnp.where(wavenumber == 0, 1.0, 2.0).astype(jnp.float32)
    return signed.astype(jnp.bfloat16), (factor[None, :] * signed).T.astype(jnp.bfloat16)


def mode_divisor(mode_rates, degree_count):
    degrees = jnp.arange(degree_count, dtype=jnp.float32)
    degree_ratio = degrees * (degrees + 1.0) / (degree_count * (degree_count + 1.0))
    return 1.0 + mode_rates[:, None] * degree_ratio[None, :]


def widen(values):
    return lax.optimization_barrier(values).astype(jnp.float32)


def grid_section(state_grid, mixing, lat_scale, forward):
    level_count, row_count, col_count = state_grid.shape
    rounded = widen(state_grid.astype(jnp.bfloat16))
    mixing_term = jnp.dot(mixing.astype(jnp.float32), rounded.reshape(level_count, row_count * col_count),
                          precision=lax.Precision.HIGHEST).reshape(level_count, row_count, col_count)
    tendency = state_grid + time_step * (mixing_term - cubic_rate * state_grid * state_grid * state_grid)
    grid_rounded = widen(tendency.astype(jnp.bfloat16)).reshape(level_count * row_count, col_count)
    fourier_sums = jnp.dot(grid_rounded, forward.astype(jnp.float32), precision=lax.Precision.HIGHEST)
    fourier_sums = fourier_sums.reshape(level_count, row_count, forward.shape[1])
    return (fourier_sums * lat_scale[None, :, None]).astype(jnp.bfloat16)


def implicit_solve(spectral, to_modes, from_modes, divisor):
    modal = jnp.einsum("kl,pmln->pmkn", to_modes, spectral, precision=lax.Precision.HIGHEST) / divisor[None, None]
    return jnp.einsum("lk,pmkn->pmln", from_modes, modal, precision=lax.Precision.HIGHEST).astype(jnp.bfloat16)


def reference(ensemble, counts, mixing, weights, legendre, to_modes, from_modes, mode_rates):
    total_waves = legendre.shape[0]
    columns = jnp.arange(2 * total_waves, dtype=jnp.int32)
    wavenumber = columns % total_waves
    component = columns // total_waves
    forward, backward = fourier_tables(wavenumber, component, NLON)
    backward_wide = backward.astype(jnp.float32)
    lat_scale = weights / NLON
    divisor = mode_divisor(mode_rates, NTOT)
    sources = clone_sources(counts)
    legendre_wide = legendre.astype(jnp.float32)

    def advance(member_index):
        state_grid = jnp.take(ensemble, member_index, axis=0)
        for timestep in range(2):
            coefficients = grid_section(state_grid, mixing, lat_scale, forward)
            split_parts = widen(coefficients).reshape(LEV, NLAT, 2, total_waves)
            spectral = jnp.einsum("ljpm,mjn->pmln", split_parts, legendre_wide, precision=lax.Precision.HIGHEST)
            implicit = widen(implicit_solve(spectral, to_modes, from_modes, divisor))
            band_parts = jnp.einsum("mjn,pmln->ljpm", legendre_wide, implicit, precision=lax.Precision.HIGHEST)
            band_parts = widen(band_parts.astype(jnp.bfloat16)).reshape(LEV * NLAT, 2 * total_waves)
            state_grid = jnp.dot(band_parts, backward_wide, precision=lax.Precision.HIGHEST).reshape(LEV, NLAT, NLON)
        return state_grid

    return lax.map(advance, sources)
```

```python
import math

import jax
import jax.numpy as jnp
from jax import lax
from jax.sharding import PartitionSpec as P

time_step = 0.3
cubic_rate = 0.1


def clone_sources(counts):
    living = (counts > 0).astype(jnp.int32)
    surplus_end = jnp.cumsum(jnp.maximum(counts - 1, 0), dtype=jnp.int32)
    killed_rank = jnp.cumsum(1 - living, dtype=jnp.int32) - (1 - living)
    pulled = jnp.sum(
        (surplus_end[None, :] <= killed_rank[:, None]).astype(jnp.int32), axis=1, dtype=jnp.int32
    )
    members = jnp.arange(counts.shape[0], dtype=jnp.int32)
    return jnp.where(living > 0, members, pulled)


def fourier_tables(wavenumber, component, longitudes):
    positions = jnp.arange(longitudes, dtype=jnp.int32)
    product_index = positions[:, None] * wavenumber[None, :] % longitudes
    angles = 2.0 * math.pi / longitudes * product_index.astype(jnp.float32)
    signed = jnp.where(component[None, :] == 0, jnp.cos(angles), -jnp.sin(angles))
    factor = jnp.where(wavenumber == 0, 1.0, 2.0).astype(jnp.float32)
    return (signed.astype(jnp.bfloat16), (factor[None, :] * signed).T.astype(jnp.bfloat16))


def mode_divisor(mode_rates, degree_count):
    degrees = jnp.arange(degree_count, dtype=jnp.float32)
    degree_ratio = degrees * (degrees + 1.0) / (degree_count * (degree_count + 1.0))
    return 1.0 + mode_rates[:, None] * degree_ratio[None, :]


def grid_section(state_grid, mixing, lat_scale, forward):
    level_count, row_count, col_count = state_grid.shape
    rounded = state_grid.astype(jnp.bfloat16)
    mixing_term = jnp.dot(
        mixing,
        rounded.reshape(level_count, row_count * col_count),
        preferred_element_type=jnp.float32,
    ).reshape(level_count, row_count, col_count)
    tendency = state_grid + time_step * (
        mixing_term - cubic_rate * state_grid * state_grid * state_grid
    )
    grid_rounded = tendency.astype(jnp.bfloat16).reshape(level_count * row_count, col_count)
    fourier_sums = jnp.dot(grid_rounded, forward, preferred_element_type=jnp.float32)
    fourier_sums = fourier_sums.reshape(level_count, row_count, forward.shape[1])
    return (fourier_sums * lat_scale[None, :, None]).astype(jnp.bfloat16)


def implicit_solve(spectral, to_modes, from_modes, divisor):
    modal = (
        jnp.einsum("kl,pmln->pmkn", to_modes, spectral, precision=lax.Precision.HIGHEST)
        / divisor[None, None]
    )
    return jnp.einsum("lk,pmkn->pmln", from_modes, modal, precision=lax.Precision.HIGHEST).astype(
        jnp.bfloat16
    )


def local(ensemble, counts, mixing, weights, legendre, to_modes, from_modes, mode_rates):
    traj_count = lax.axis_size("traj")
    lat_count = lax.axis_size("lat")
    local_waves = legendre.shape[0]
    degree_count = legendre.shape[2]
    total_waves = local_waves * lat_count
    longitudes = ensemble.shape[3]
    columns = jnp.arange(2 * total_waves, dtype=jnp.int32)
    within = columns % (2 * local_waves)
    wavenumber = columns // (2 * local_waves) * local_waves + within % local_waves
    component = within // local_waves
    forward, backward = fourier_tables(wavenumber, component, longitudes)
    lat_scale = weights / longitudes
    divisor = mode_divisor(mode_rates, degree_count)

    def to_spectral(received):
        split_parts = received.reshape(received.shape[0], received.shape[1], 2, local_waves)
        return jnp.einsum(
            "ljpm,mjn->pmln", split_parts, legendre, preferred_element_type=jnp.float32
        )

    def to_grid(received):
        flat_rows = received.reshape(received.shape[0] * received.shape[1], received.shape[2])
        result_grid = jnp.dot(flat_rows, backward, preferred_element_type=jnp.float32)
        return result_grid.reshape(received.shape[0], received.shape[1], longitudes)

    def to_implicit(coefficients):
        spectral = to_spectral(
            lax.all_to_all(coefficients, "lat", split_axis=2, concat_axis=1, tiled=True)
        )
        return implicit_solve(spectral, to_modes, from_modes, divisor)

    def to_band_grid(implicit):
        band_parts = jnp.einsum(
            "mjn,pmln->ljpm", legendre, implicit, preferred_element_type=jnp.float32
        )
        band_parts = band_parts.astype(jnp.bfloat16)
        band_parts = band_parts.reshape(band_parts.shape[0], band_parts.shape[1], 2 * local_waves)
        return to_grid(lax.all_to_all(band_parts, "lat", split_axis=1, concat_axis=2, tiled=True))

    state_grid = ensemble[0]
    own_implicit = to_implicit(grid_section(state_grid, mixing, lat_scale, forward))
    pieces = own_implicit.reshape(traj_count, own_implicit.size // traj_count // 128, 128)
    marker = jnp.broadcast_to(counts.astype(jnp.bfloat16)[:, None, None], (traj_count, 4, 128))
    spread = lax.all_to_all(
        jnp.concatenate([pieces, marker], axis=1), "traj", split_axis=0, concat_axis=0, tiled=True
    )
    piece_rows = pieces.shape[1]
    sources = clone_sources(spread[:, piece_rows, 0].astype(jnp.int32))
    chosen = jnp.take(spread, sources, axis=0)
    implicit = lax.all_to_all(chosen, "traj", split_axis=0, concat_axis=0, tiled=True)
    implicit = implicit[:, :piece_rows].reshape(own_implicit.shape)
    state_grid = to_band_grid(implicit)
    state_grid = to_band_grid(to_implicit(grid_section(state_grid, mixing, lat_scale, forward)))
    return state_grid[None]


def solution(mesh):
    placed = (
        P("traj", None, "lat", None),
        P("traj"),
        P(),
        P("lat"),
        P("lat", None, None),
        P(),
        P(),
        P(),
    )
    return jax.shard_map(
        local, mesh=mesh, in_specs=placed, out_specs=P("traj", None, "lat", None), check_vma=False
    )
```

```python
import math

import jax
import jax.numpy as jnp
from jax import lax
from jax.experimental import pallas as pl
from jax.experimental.pallas import tpu as pltpu
from jax.sharding import PartitionSpec as P

time_step = 0.3
cubic_rate = 0.1


def fourier_tables(wavenumber, component, longitudes):
    positions = jnp.arange(longitudes, dtype=jnp.int32)
    product_index = positions[:, None] * wavenumber[None, :] % longitudes
    angles = 2.0 * math.pi / longitudes * product_index.astype(jnp.float32)
    signed = jnp.where(component[None, :] == 0, jnp.cos(angles), -jnp.sin(angles))
    factor = jnp.where(wavenumber == 0, 1.0, 2.0).astype(jnp.float32)
    return (signed.astype(jnp.bfloat16), (factor[None, :] * signed).T.astype(jnp.bfloat16))


def mode_divisor(mode_rates, degree_count):
    degrees = jnp.arange(degree_count, dtype=jnp.float32)
    degree_ratio = degrees * (degrees + 1.0) / (degree_count * (degree_count + 1.0))
    return 1.0 + mode_rates[:, None] * degree_ratio[None, :]


def grid_tendency(state_grid, mixing):
    level_count, row_count, col_count = state_grid.shape
    rounded = state_grid.astype(jnp.bfloat16)
    mixing_term = jnp.dot(
        mixing,
        rounded.reshape(level_count, row_count * col_count),
        preferred_element_type=jnp.float32,
    ).reshape(level_count, row_count, col_count)
    tendency = state_grid + time_step * (
        mixing_term - cubic_rate * state_grid * state_grid * state_grid
    )
    return tendency.astype(jnp.bfloat16)


def mix_levels(matrix, grid):
    level_count, row_count, col_count = grid.shape
    flat = grid.reshape(level_count, row_count * col_count)
    mixed = jnp.dot(matrix.astype(jnp.bfloat16), flat, preferred_element_type=jnp.float32)
    return mixed.reshape(grid.shape)


def grid_section(state_grid, mixing, lat_scale, forward):
    level_count, row_count, col_count = state_grid.shape
    grid_rounded = grid_tendency(state_grid, mixing).reshape(level_count * row_count, col_count)
    fourier_sums = jnp.dot(grid_rounded, forward, preferred_element_type=jnp.float32)
    fourier_sums = fourier_sums.reshape(level_count, row_count, forward.shape[1])
    return (fourier_sums * lat_scale[None, :, None]).astype(jnp.bfloat16)


def contract(left, right, left_dim, right_dim):
    return lax.dot_general(
        left, right, (((left_dim,), (right_dim,)), ((), ())), preferred_element_type=jnp.float32
    )


def block_mask(rows, cols, test):
    row = lax.broadcasted_iota(jnp.int32, (rows, cols), 0)
    col = lax.broadcasted_iota(jnp.int32, (rows, cols), 1)
    return test(row, col)


def spread_kernel(count_ref, table_ref, grid_ref, scale_ref, out_ref):
    wave_count, quarters, pair_rows, lanes = out_ref.shape
    used = grid_ref.shape[0] // quarters
    table = table_ref[...]
    lane = lax.broadcasted_iota(jnp.int32, (wave_count * pair_rows, lanes), 1)
    for quarter in range(quarters):
        block = grid_ref[quarter * used : (quarter + 1) * used, :]
        block = jnp.concatenate(
            [block, jnp.zeros((lanes - used, block.shape[1]), block.dtype)], axis=0
        )
        sums = contract(table, block, 1, 1) * scale_ref[...]
        sums = jnp.where(lane < used, sums, count_ref[0])
        out_ref[:, quarter] = sums.astype(jnp.bfloat16).reshape(wave_count, pair_rows, lanes)


def selection(count_row, size):
    surplus = jnp.maximum(count_row - 1.0, 0.0).astype(jnp.bfloat16)
    dead = jnp.where(count_row == 0.0, 1.0, 0.0).astype(jnp.bfloat16)
    dead_all = jnp.broadcast_to(dead[0:1], (size, size))
    surplus_all = jnp.broadcast_to(surplus[0:1], (size, size))

    def ones_where(test):
        return jnp.where(block_mask(size, size, test), 1.0, 0.0).astype(jnp.bfloat16)

    upto = ones_where(lambda r, c: (r // 2 <= c // 2) & (r % 2 == 0))
    before = ones_where(lambda r, c: (c // 2 < r // 2) & (c % 2 == 0))
    same = ones_where(lambda r, c: r == c)
    surplus_end = contract(surplus_all, upto, 1, 0)
    killed_rank = contract(before, dead_all, 1, 1)
    killed = contract(same, dead_all, 1, 1)
    even = block_mask(size, size, lambda r, c: c % 2 == 0)
    pulled = jnp.sum(
        jnp.where(even & (surplus_end <= killed_rank), 1.0, 0.0), axis=1, keepdims=True
    )
    member = lax.broadcasted_iota(jnp.int32, (size, size), 0) // 2
    source = jnp.where(killed > 0.5, jnp.broadcast_to(pulled, (size, size)), member.astype(jnp.float32))
    picked = lax.broadcasted_iota(jnp.int32, (size, size), 1) // 2
    parity = block_mask(size, size, lambda r, c: r % 2 == c % 2)
    return jnp.where(parity & (picked.astype(jnp.float32) == source), 1.0, 0.0).astype(jnp.bfloat16)


def wave_kernel(parts_ref, table_ref, turned_ref, inverse_ref, out_ref, wave_ref, band_ref):
    lat_count, size, lanes = parts_ref.shape
    modes, lat_rows, _ = wave_ref.shape
    rows = lat_rows // lat_count
    used = modes * rows
    unit = jnp.where(block_mask(used + 8, lanes, lambda r, c: r == c), 1.0, 0.0).astype(jnp.bfloat16)
    pick = None
    for lat in range(lat_count):
        turned = contract(unit, parts_ref[lat], 1, 1)
        if lat == 0:
            pick = selection(turned[used : used + 8], size)
        for mode in range(modes):
            wave_ref[mode, lat * rows : (lat + 1) * rows, :] = turned[mode * rows : (mode + 1) * rows]
    table = table_ref[...]
    turned_table = turned_ref[...]
    for mode in range(modes):
        spectral = contract(turned_table, wave_ref[mode].astype(jnp.bfloat16), 1, 0)
        modal = (spectral * inverse_ref[:, mode : mode + 1]).astype(jnp.bfloat16)
        band = contract(table, modal, 1, 0)
        for lat in range(lat_count):
            band_ref[lat, mode * rows : (mode + 1) * rows, :] = band[lat * rows : (lat + 1) * rows]
    out_ref[...] = jnp.zeros(out_ref.shape, out_ref.dtype)
    for lat in range(lat_count):
        chosen = contract(pick, band_ref[lat].astype(jnp.bfloat16), 1, 1)
        out_ref[lat, :, 0:used] = chosen.astype(jnp.bfloat16)


def gather_kernel(parts_ref, table_ref, out_ref):
    quarters = parts_ref.shape[0]
    used = out_ref.shape[0] // quarters
    for quarter in range(quarters):
        sums = contract(parts_ref[quarter], table_ref[...], 0, 0)
        out_ref[quarter * used : (quarter + 1) * used, :] = sums[:used].astype(jnp.bfloat16)


def implicit_solve(spectral, to_modes, from_modes, divisor):
    modal = (
        jnp.einsum("kl,pmln->pmkn", to_modes, spectral, precision=lax.Precision.HIGHEST)
        / divisor[None, None]
    )
    return jnp.einsum("lk,pmkn->pmln", from_modes, modal, precision=lax.Precision.HIGHEST).astype(
        jnp.bfloat16
    )


def local(ensemble, counts, mixing, weights, legendre, to_modes, from_modes, mode_rates):
    traj_count = lax.axis_size("traj")
    lat_count = lax.axis_size("lat")
    local_waves = legendre.shape[0]
    degree_count = legendre.shape[2]
    total_waves = local_waves * lat_count
    longitudes = ensemble.shape[3]
    columns = jnp.arange(2 * total_waves, dtype=jnp.int32)
    within = columns % (2 * local_waves)
    wavenumber = columns // (2 * local_waves) * local_waves + within % local_waves
    component = within // local_waves
    forward, backward = fourier_tables(wavenumber, component, longitudes)
    lat_scale = weights / longitudes
    divisor = mode_divisor(mode_rates, degree_count)
    vmem = pl.BlockSpec(memory_space=pltpu.VMEM)
    smem = pl.BlockSpec(memory_space=pltpu.SMEM)

    def to_spectral(received):
        split_parts = received.reshape(received.shape[0], received.shape[1], 2, local_waves)
        return jnp.einsum(
            "ljpm,mjn->pmln", split_parts, legendre, preferred_element_type=jnp.float32
        )

    def to_grid(received):
        flat_rows = received.reshape(received.shape[0] * received.shape[1], received.shape[2])
        result_grid = jnp.dot(flat_rows, backward, preferred_element_type=jnp.float32)
        return result_grid.reshape(received.shape[0], received.shape[1], longitudes)

    def to_implicit(coefficients):
        spectral = to_spectral(
            lax.all_to_all(coefficients, "lat", split_axis=2, concat_axis=1, tiled=True)
        )
        return implicit_solve(spectral, to_modes, from_modes, divisor)

    def to_band_grid(implicit):
        band_parts = jnp.einsum(
            "mjn,pmln->ljpm", legendre, implicit, preferred_element_type=jnp.float32
        )
        band_parts = band_parts.astype(jnp.bfloat16)
        band_parts = band_parts.reshape(band_parts.shape[0], band_parts.shape[1], 2 * local_waves)
        return to_grid(lax.all_to_all(band_parts, "lat", split_axis=1, concat_axis=2, tiled=True))

    level_count, row_count = ensemble.shape[1], ensemble.shape[2]
    quarters = traj_count // local_waves
    modes = level_count // quarters
    used = modes * row_count
    lanes = -(-(used + 1) // 128) * 128
    pairs = jnp.arange(2 * total_waves, dtype=jnp.int32)
    pair_wave = pairs // 2 % lat_count * local_waves + pairs // (2 * lat_count)
    pair_forward, pair_backward = fourier_tables(pair_wave, pairs % 2, longitudes)
    traj_index = lax.axis_index("traj")
    own_table = lax.dynamic_index_in_dim(legendre, traj_index // quarters, 0, keepdims=False)
    own_divisor = lax.dynamic_slice_in_dim(divisor, traj_index % quarters * modes, modes, 0)
    own_inverse = (1.0 / own_divisor).T
    lane_scale = jnp.pad(jnp.tile(lat_scale, modes), (0, lanes - used))[None, :]

    grid_rounded = grid_tendency(ensemble[0], mixing)
    modal_grid = mix_levels(to_modes, grid_rounded).astype(jnp.bfloat16)
    outgoing = pl.pallas_call(
        spread_kernel,
        out_shape=jax.ShapeDtypeStruct(
            (local_waves, quarters, 2 * lat_count, lanes), jnp.bfloat16
        ),
        in_specs=[smem, vmem, vmem, vmem],
        out_specs=vmem,
        name="spread_fourier",
    )(
        counts.astype(jnp.float32),
        pair_forward.T,
        modal_grid.reshape(level_count * row_count, longitudes),
        lane_scale,
    )
    everyone = ("traj", "lat")
    arrived = lax.all_to_all(
        outgoing.reshape(traj_count * lat_count, 2, lanes), everyone, 0, 0, tiled=True
    )
    arrived = arrived.reshape(traj_count, lat_count, 2, lanes).transpose(1, 0, 2, 3)
    band_parts = pl.pallas_call(
        wave_kernel,
        out_shape=jax.ShapeDtypeStruct((lat_count, 2 * traj_count, lanes), jnp.bfloat16),
        in_specs=[vmem, vmem, vmem, vmem],
        out_specs=vmem,
        scratch_shapes=[
            pltpu.VMEM((modes, lat_count * row_count, 2 * traj_count), jnp.float32),
            pltpu.VMEM((lat_count, used, 2 * traj_count), jnp.float32),
        ],
        name="wave_solve",
    )(
        arrived.reshape(lat_count, 2 * traj_count, lanes),
        own_table,
        own_table.T,
        own_inverse,
    )
    band_parts = band_parts.reshape(lat_count, traj_count, 2, lanes).transpose(1, 0, 2, 3)
    returned = lax.all_to_all(
        band_parts.reshape(traj_count * lat_count, 2, lanes), everyone, 0, 0, tiled=True
    )
    returned = returned.reshape(local_waves, quarters, 2 * lat_count, lanes).transpose(1, 0, 2, 3)
    modal_grid = pl.pallas_call(
        gather_kernel,
        out_shape=jax.ShapeDtypeStruct((level_count * row_count, longitudes), jnp.bfloat16),
        in_specs=[vmem, vmem],
        out_specs=vmem,
        name="gather_fourier",
    )(returned.reshape(quarters, 2 * total_waves, lanes), pair_backward)
    state_grid = mix_levels(from_modes, modal_grid.reshape(level_count, row_count, longitudes))
    state_grid = to_band_grid(to_implicit(grid_section(state_grid, mixing, lat_scale, forward)))
    return state_grid[None]


def solution(mesh):
    placed = (
        P("traj", None, "lat", None),
        P("traj"),
        P(),
        P("lat"),
        P("lat", None, None),
        P(),
        P(),
        P(),
    )
    return jax.shard_map(
        local, mesh=mesh, in_specs=placed, out_specs=P("traj", None, "lat", None), check_vma=False
    )
```

```python
import math

import jax
import jax.numpy as jnp
import numpy as np
from jax import lax
from jax.experimental import pallas as pl
from jax.experimental.pallas import tpu as pltpu
from jax.sharding import PartitionSpec as P

time_step = 0.3
cubic_rate = 0.1


def fourier_tables(wavenumber, component, longitudes):
    positions = np.arange(longitudes)
    product_index = positions[:, None] * wavenumber[None, :] % longitudes
    angles = 2.0 * math.pi / longitudes * product_index
    signed = np.where(component[None, :] == 0, np.cos(angles), -np.sin(angles))
    factor = np.where(wavenumber == 0, 1.0, 2.0)
    rounded = jnp.bfloat16
    return signed.astype(rounded), (factor[None, :] * signed).T.astype(rounded)


def mode_divisor(mode_rates, degree_count):
    degrees = jnp.arange(degree_count, dtype=jnp.float32)
    degree_ratio = degrees * (degrees + 1.0) / (degree_count * (degree_count + 1.0))
    return 1.0 + mode_rates[:, None] * degree_ratio[None, :]


def grid_tendency(state_grid, mixing):
    level_count, row_count, col_count = state_grid.shape
    rounded = state_grid.astype(jnp.bfloat16)
    mixing_term = jnp.dot(
        mixing,
        rounded.reshape(level_count, row_count * col_count),
        preferred_element_type=jnp.float32,
    ).reshape(level_count, row_count, col_count)
    tendency = state_grid + time_step * (
        mixing_term - cubic_rate * state_grid * state_grid * state_grid
    )
    return tendency.astype(jnp.bfloat16)


def mix_levels(matrix, grid):
    level_count, row_count, col_count = grid.shape
    flat = grid.reshape(level_count, row_count * col_count)
    mixed = jnp.dot(matrix.astype(jnp.bfloat16), flat, preferred_element_type=jnp.float32)
    return mixed.reshape(grid.shape)


def grid_section(state_grid, mixing, lat_scale, forward):
    level_count, row_count, col_count = state_grid.shape
    grid_rounded = grid_tendency(state_grid, mixing).reshape(level_count * row_count, col_count)
    fourier_sums = jnp.dot(grid_rounded, forward, preferred_element_type=jnp.float32)
    fourier_sums = fourier_sums.reshape(level_count, row_count, forward.shape[1])
    return (fourier_sums * lat_scale[None, :, None]).astype(jnp.bfloat16)


def contract(left, right, left_dim, right_dim):
    return lax.dot_general(
        left, right, (((left_dim,), (right_dim,)), ((), ())), preferred_element_type=jnp.float32
    )


def block_mask(rows, cols, test):
    row = lax.broadcasted_iota(jnp.int32, (rows, cols), 0)
    col = lax.broadcasted_iota(jnp.int32, (rows, cols), 1)
    return test(row, col)


def spread_kernel(count_ref, table_ref, grid_ref, out_ref):
    wave_count, quarters, lat_count, _, lanes = out_ref.shape
    used = grid_ref.shape[0] // quarters
    table = table_ref[...]
    lane = lax.broadcasted_iota(jnp.int32, table.shape[:1] + (lanes,), 1)
    for quarter in range(quarters):
        block = grid_ref[quarter * used : (quarter + 1) * used, :]
        block = jnp.concatenate(
            [block, jnp.zeros((lanes - used, block.shape[1]), block.dtype)], axis=0
        )
        sums = contract(table, block, 1, 1)
        sums = jnp.where(lane < used, sums, count_ref[0])
        out_ref[:, quarter] = sums.astype(jnp.bfloat16).reshape(wave_count, lat_count, 2, lanes)


def selection(count_row, size):
    surplus = jnp.maximum(count_row - 1.0, 0.0).astype(jnp.bfloat16)
    dead = jnp.where(count_row == 0.0, 1.0, 0.0).astype(jnp.bfloat16)
    dead_all = jnp.broadcast_to(dead[0:1], (size, size))
    surplus_all = jnp.broadcast_to(surplus[0:1], (size, size))

    def ones_where(test):
        return jnp.where(block_mask(size, size, test), 1.0, 0.0).astype(jnp.bfloat16)

    upto = ones_where(lambda r, c: (r // 2 <= c // 2) & (r % 2 == 0))
    before = ones_where(lambda r, c: (c // 2 < r // 2) & (c % 2 == 0))
    same = ones_where(lambda r, c: r == c)
    surplus_end = contract(surplus_all, upto, 1, 0)
    killed_rank = contract(before, dead_all, 1, 1)
    killed = contract(same, dead_all, 1, 1)
    even = block_mask(size, size, lambda r, c: c % 2 == 0)
    pulled = jnp.sum(
        jnp.where(even & (surplus_end <= killed_rank), 1.0, 0.0), axis=1, keepdims=True
    )
    member = lax.broadcasted_iota(jnp.int32, (size, size), 0) // 2
    source = jnp.where(killed > 0.5, jnp.broadcast_to(pulled, (size, size)), member.astype(jnp.float32))
    picked = lax.broadcasted_iota(jnp.int32, (size, size), 1) // 2
    parity = block_mask(size, size, lambda r, c: r % 2 == c % 2)
    return jnp.where(parity & (picked.astype(jnp.float32) == source), 1.0, 0.0).astype(jnp.bfloat16)


def wave_kernel(parts_ref, table_ref, turned_ref, inverse_ref, out_ref, wave_ref, band_ref):
    members, lat_count, _, lanes = parts_ref.shape
    size = 2 * members
    modes, lat_rows, _ = wave_ref.shape
    rows = lat_rows // lat_count
    used = modes * rows
    unit = jnp.where(block_mask(used + 8, lanes, lambda r, c: r == c), 1.0, 0.0).astype(jnp.bfloat16)
    pick = None
    for lat in range(lat_count):
        turned = contract(unit, parts_ref[:, lat].reshape(size, lanes), 1, 1)
        if lat == 0:
            pick = selection(turned[used : used + 8], size)
        for mode in range(modes):
            wave_ref[mode, lat * rows : (lat + 1) * rows, :] = turned[mode * rows : (mode + 1) * rows]
    table = table_ref[...]
    turned_table = turned_ref[...]
    for mode in range(modes):
        spectral = contract(turned_table, wave_ref[mode].astype(jnp.bfloat16), 1, 0)
        modal = (spectral * inverse_ref[:, mode : mode + 1]).astype(jnp.bfloat16)
        band = contract(table, modal, 1, 0)
        for lat in range(lat_count):
            band_ref[lat, mode * rows : (mode + 1) * rows, :] = band[lat * rows : (lat + 1) * rows]
    spare = jnp.zeros((lanes - used, band_ref.shape[2]), jnp.bfloat16)
    for lat in range(lat_count):
        band = jnp.concatenate([band_ref[lat].astype(jnp.bfloat16), spare], axis=0)
        chosen = contract(pick, band, 1, 1).astype(jnp.bfloat16)
        out_ref[:, lat] = chosen.reshape(members, 2, lanes)


def gather_kernel(parts_ref, table_ref, out_ref):
    _, quarters, _, _, lanes = parts_ref.shape
    used = out_ref.shape[0] // quarters
    for quarter in range(quarters):
        sums = contract(
            parts_ref[:, quarter].reshape(table_ref.shape[0], lanes), table_ref[...], 0, 0
        )
        out_ref[quarter * used : (quarter + 1) * used, :] = sums[:used].astype(jnp.bfloat16)


def implicit_solve(spectral, to_modes, from_modes, divisor):
    modal = (
        jnp.einsum("kl,pmln->pmkn", to_modes, spectral, precision=lax.Precision.HIGHEST)
        / divisor[None, None]
    )
    return jnp.einsum("lk,pmkn->pmln", from_modes, modal, precision=lax.Precision.HIGHEST).astype(
        jnp.bfloat16
    )


def local(ensemble, counts, mixing, weights, legendre, to_modes, from_modes, mode_rates):
    traj_count = lax.axis_size("traj")
    lat_count = lax.axis_size("lat")
    local_waves = legendre.shape[0]
    degree_count = legendre.shape[2]
    total_waves = local_waves * lat_count
    longitudes = ensemble.shape[3]
    columns = np.arange(2 * total_waves)
    within = columns % (2 * local_waves)
    wavenumber = columns // (2 * local_waves) * local_waves + within % local_waves
    component = within // local_waves
    forward, backward = fourier_tables(wavenumber, component, longitudes)
    lat_scale = weights / longitudes
    divisor = mode_divisor(mode_rates, degree_count)
    vmem = pl.BlockSpec(memory_space=pltpu.VMEM)
    smem = pl.BlockSpec(memory_space=pltpu.SMEM)

    def to_spectral(received):
        split_parts = received.reshape(received.shape[0], received.shape[1], 2, local_waves)
        return jnp.einsum(
            "ljpm,mjn->pmln", split_parts, legendre, preferred_element_type=jnp.float32
        )

    def to_grid(received):
        flat_rows = received.reshape(received.shape[0] * received.shape[1], received.shape[2])
        result_grid = jnp.dot(flat_rows, backward, preferred_element_type=jnp.float32)
        return result_grid.reshape(received.shape[0], received.shape[1], longitudes)

    def to_implicit(coefficients):
        spectral = to_spectral(
            lax.all_to_all(coefficients, "lat", split_axis=2, concat_axis=1, tiled=True)
        )
        return implicit_solve(spectral, to_modes, from_modes, divisor)

    def to_band_grid(implicit):
        band_parts = jnp.einsum(
            "mjn,pmln->ljpm", legendre, implicit, preferred_element_type=jnp.float32
        )
        band_parts = band_parts.astype(jnp.bfloat16)
        band_parts = band_parts.reshape(band_parts.shape[0], band_parts.shape[1], 2 * local_waves)
        return to_grid(lax.all_to_all(band_parts, "lat", split_axis=1, concat_axis=2, tiled=True))

    level_count, row_count = ensemble.shape[1], ensemble.shape[2]
    quarters = traj_count // local_waves
    modes = level_count // quarters
    used = modes * row_count
    lanes = -(-(used + 1) // 128) * 128
    pairs = np.arange(2 * total_waves)
    pair_wave = pairs // 2 % lat_count * local_waves + pairs // (2 * lat_count)
    pair_forward, pair_backward = fourier_tables(pair_wave, pairs % 2, longitudes)
    traj_index = lax.axis_index("traj")
    own_table = lax.dynamic_index_in_dim(legendre, traj_index // quarters, 0, keepdims=False)
    own_divisor = lax.dynamic_slice_in_dim(divisor, traj_index % quarters * modes, modes, 0)
    own_inverse = (1.0 / own_divisor).T

    grid_rounded = grid_tendency(ensemble[0], mixing)
    modal_grid = mix_levels(to_modes, grid_rounded) * lat_scale[None, :, None]
    modal_grid = modal_grid.astype(jnp.bfloat16)
    outgoing = pl.pallas_call(
        spread_kernel,
        out_shape=jax.ShapeDtypeStruct(
            (local_waves, quarters, lat_count, 2, lanes), jnp.bfloat16
        ),
        in_specs=[smem, vmem, vmem],
        out_specs=vmem,
        name="spread_fourier",
    )(
        counts.astype(jnp.float32),
        np.ascontiguousarray(pair_forward.T),
        modal_grid.reshape(level_count * row_count, longitudes),
    )
    everyone = ("traj", "lat")
    arrived = lax.all_to_all(
        outgoing.reshape(traj_count * lat_count, 2, lanes), everyone, 0, 0, tiled=True
    )
    band_parts = pl.pallas_call(
        wave_kernel,
        out_shape=jax.ShapeDtypeStruct((traj_count, lat_count, 2, lanes), jnp.bfloat16),
        in_specs=[vmem, vmem, vmem, vmem],
        out_specs=vmem,
        scratch_shapes=[
            pltpu.VMEM((modes, lat_count * row_count, 2 * traj_count), jnp.float32),
            pltpu.VMEM((lat_count, used, 2 * traj_count), jnp.float32),
        ],
        name="wave_solve",
    )(
        arrived.reshape(traj_count, lat_count, 2, lanes),
        own_table,
        own_table.T,
        own_inverse,
    )
    returned = lax.all_to_all(
        band_parts.reshape(traj_count * lat_count, 2, lanes), everyone, 0, 0, tiled=True
    )
    modal_grid = pl.pallas_call(
        gather_kernel,
        out_shape=jax.ShapeDtypeStruct((level_count * row_count, longitudes), jnp.bfloat16),
        in_specs=[vmem, vmem],
        out_specs=vmem,
        name="gather_fourier",
    )(returned.reshape(local_waves, quarters, lat_count, 2, lanes), pair_backward)
    state_grid = mix_levels(from_modes, modal_grid.reshape(level_count, row_count, longitudes))
    state_grid = to_band_grid(to_implicit(grid_section(state_grid, mixing, lat_scale, forward)))
    return state_grid[None]


def solution(mesh):
    placed = (
        P("traj", None, "lat", None),
        P("traj"),
        P(),
        P("lat"),
        P("lat", None, None),
        P(),
        P(),
        P(),
    )
    return jax.shard_map(
        local, mesh=mesh, in_specs=placed, out_specs=P("traj", None, "lat", None), check_vma=False
    )
```

```python
import math

import jax
import jax.numpy as jnp
import numpy as np
from jax import lax
from jax.experimental import pallas as pl
from jax.experimental.pallas import tpu as pltpu
from jax.sharding import PartitionSpec as P

time_step = 0.3
cubic_rate = 0.1


def fourier_tables(wavenumber, component, longitudes):
    positions = np.arange(longitudes)
    product_index = positions[:, None] * wavenumber[None, :] % longitudes
    angles = 2.0 * math.pi / longitudes * product_index
    signed = np.where(component[None, :] == 0, np.cos(angles), -np.sin(angles))
    factor = np.where(wavenumber == 0, 1.0, 2.0)
    rounded = jnp.bfloat16
    return signed.astype(rounded), (factor[None, :] * signed).T.astype(rounded)


def mode_divisor(mode_rates, degree_count):
    degrees = jnp.arange(degree_count, dtype=jnp.float32)
    degree_ratio = degrees * (degrees + 1.0) / (degree_count * (degree_count + 1.0))
    return 1.0 + mode_rates[:, None] * degree_ratio[None, :]


def grid_tendency(state_grid, mixing):
    level_count, row_count, col_count = state_grid.shape
    rounded = state_grid.astype(jnp.bfloat16)
    mixing_term = jnp.dot(
        mixing,
        rounded.reshape(level_count, row_count * col_count),
        preferred_element_type=jnp.float32,
    ).reshape(level_count, row_count, col_count)
    tendency = state_grid + time_step * (
        mixing_term - cubic_rate * state_grid * state_grid * state_grid
    )
    return tendency.astype(jnp.bfloat16)


def mix_levels(matrix, grid):
    level_count, row_count, col_count = grid.shape
    flat = grid.reshape(level_count, row_count * col_count)
    mixed = jnp.dot(matrix.astype(jnp.bfloat16), flat, preferred_element_type=jnp.float32)
    return mixed.reshape(grid.shape)


def grid_section(state_grid, mixing, lat_scale, forward):
    level_count, row_count, col_count = state_grid.shape
    grid_rounded = grid_tendency(state_grid, mixing).reshape(level_count * row_count, col_count)
    fourier_sums = jnp.dot(grid_rounded, forward, preferred_element_type=jnp.float32)
    fourier_sums = fourier_sums.reshape(level_count, row_count, forward.shape[1])
    return (fourier_sums * lat_scale[None, :, None]).astype(jnp.bfloat16)


def contract(left, right, left_dim, right_dim):
    return lax.dot_general(
        left, right, (((left_dim,), (right_dim,)), ((), ())), preferred_element_type=jnp.float32
    )


def block_mask(rows, cols, test):
    row = lax.broadcasted_iota(jnp.int32, (rows, cols), 0)
    col = lax.broadcasted_iota(jnp.int32, (rows, cols), 1)
    return test(row, col)


def first_kernel(
    count_ref, weight_ref, table_ref, mixing_ref, to_ref, grid_ref, out_ref, modal_ref
):
    level_count, row_count, longitudes = grid_ref.shape
    wave_count, quarters, lat_count, _, lanes = out_ref.shape
    modes = level_count // quarters
    used = modes * row_count
    mixing, to_modes = mixing_ref[...], to_ref[...]
    for row in range(row_count):
        state = grid_ref[:, row, :]
        mixed = contract(mixing, state.astype(jnp.bfloat16), 1, 0)
        tendency = state + time_step * (mixed - cubic_rate * state * state * state)
        modal = contract(to_modes, tendency.astype(jnp.bfloat16), 1, 0)
        modal_ref[:, row, :] = modal * (weight_ref[row] * (1.0 / longitudes))
    table = table_ref[...]
    lane = lax.broadcasted_iota(jnp.int32, table.shape[:1] + (lanes,), 1)
    spare = jnp.zeros((lanes - used, longitudes), jnp.bfloat16)
    for quarter in range(quarters):
        block = modal_ref[quarter * modes : (quarter + 1) * modes]
        block = block.reshape(used, longitudes).astype(jnp.bfloat16)
        sums = contract(table, jnp.concatenate([block, spare], axis=0), 1, 1)
        sums = jnp.where(lane < used, sums, count_ref[0]).astype(jnp.bfloat16)
        out_ref[:, quarter] = sums.reshape(wave_count, lat_count, 2, lanes)


def selection(count_row, size):
    surplus = jnp.maximum(count_row - 1.0, 0.0).astype(jnp.bfloat16)
    dead = jnp.where(count_row == 0.0, 1.0, 0.0).astype(jnp.bfloat16)
    dead_all = jnp.broadcast_to(dead[0:1], (size, size))
    surplus_all = jnp.broadcast_to(surplus[0:1], (size, size))

    def ones_where(test):
        return jnp.where(block_mask(size, size, test), 1.0, 0.0).astype(jnp.bfloat16)

    upto = ones_where(lambda r, c: (r // 2 <= c // 2) & (r % 2 == 0))
    before = ones_where(lambda r, c: (c // 2 < r // 2) & (c % 2 == 0))
    same = ones_where(lambda r, c: r == c)
    surplus_end = contract(surplus_all, upto, 1, 0)
    killed_rank = contract(before, dead_all, 1, 1)
    killed = contract(same, dead_all, 1, 1)
    even = block_mask(size, size, lambda r, c: c % 2 == 0)
    pulled = jnp.sum(
        jnp.where(even & (surplus_end <= killed_rank), 1.0, 0.0), axis=1, keepdims=True
    )
    member = lax.broadcasted_iota(jnp.int32, (size, size), 0) // 2
    source = jnp.where(killed > 0.5, jnp.broadcast_to(pulled, (size, size)), member.astype(jnp.float32))
    picked = lax.broadcasted_iota(jnp.int32, (size, size), 1) // 2
    parity = block_mask(size, size, lambda r, c: r % 2 == c % 2)
    return jnp.where(parity & (picked.astype(jnp.float32) == source), 1.0, 0.0).astype(jnp.bfloat16)


def wave_kernel(parts_ref, table_ref, turned_ref, inverse_ref, out_ref, wave_ref, band_ref):
    members, lat_count, _, lanes = parts_ref.shape
    size = 2 * members
    modes, lat_rows, _ = wave_ref.shape
    rows = lat_rows // lat_count
    used = modes * rows
    unit = jnp.where(block_mask(used + 8, lanes, lambda r, c: r == c), 1.0, 0.0).astype(jnp.bfloat16)
    pick = None
    for lat in range(lat_count):
        turned = contract(unit, parts_ref[:, lat].reshape(size, lanes), 1, 1)
        if lat == 0:
            pick = selection(turned[used : used + 8], size)
        for mode in range(modes):
            wave_ref[mode, lat * rows : (lat + 1) * rows, :] = turned[mode * rows : (mode + 1) * rows]
    table = table_ref[...]
    turned_table = turned_ref[...]
    for mode in range(modes):
        spectral = contract(turned_table, wave_ref[mode].astype(jnp.bfloat16), 1, 0)
        modal = (spectral * inverse_ref[:, mode : mode + 1]).astype(jnp.bfloat16)
        band = contract(table, modal, 1, 0)
        for lat in range(lat_count):
            band_ref[lat, mode * rows : (mode + 1) * rows, :] = band[lat * rows : (lat + 1) * rows]
    spare = jnp.zeros((lanes - used, band_ref.shape[2]), jnp.bfloat16)
    for lat in range(lat_count):
        band = jnp.concatenate([band_ref[lat].astype(jnp.bfloat16), spare], axis=0)
        chosen = contract(pick, band, 1, 1).astype(jnp.bfloat16)
        out_ref[:, lat] = chosen.reshape(members, 2, lanes)


def band_kernel(implicit_ref, legendre_ref, out_ref, band_ref):
    lat_count, columns, lanes = out_ref.shape
    _, all_rows, level_count = band_ref.shape
    rows = all_rows // lat_count
    waves = legendre_ref.shape[0]
    for column in range(columns):
        own = implicit_ref[column // waves, column % waves]
        band_ref[column] = contract(legendre_ref[column % waves], own, 1, 1)
    for lat in range(lat_count):
        for row in range(rows):
            piece = band_ref[:, lat * rows + row, :].astype(jnp.bfloat16)
            out_ref[lat, :, row * level_count : (row + 1) * level_count] = piece
    used = rows * level_count
    out_ref[:, :, used:] = jnp.zeros((lat_count, columns, lanes - used), jnp.bfloat16)


def last_kernel(parts_ref, table_ref, out_ref):
    level_count, row_count, _ = out_ref.shape
    parts = parts_ref[...].reshape(table_ref.shape[0], parts_ref.shape[2])
    sums = contract(parts, table_ref[...], 0, 0)
    for row in range(row_count):
        out_ref[:, row, :] = sums[row * level_count : (row + 1) * level_count]


def gather_kernel(parts_ref, table_ref, out_ref):
    _, quarters, _, _, lanes = parts_ref.shape
    used = out_ref.shape[0] // quarters
    for quarter in range(quarters):
        sums = contract(
            parts_ref[:, quarter].reshape(table_ref.shape[0], lanes), table_ref[...], 0, 0
        )
        out_ref[quarter * used : (quarter + 1) * used, :] = sums[:used].astype(jnp.bfloat16)


def implicit_solve(spectral, to_modes, from_modes, divisor):
    modal = (
        jnp.einsum("kl,pmln->pmkn", to_modes, spectral, precision=lax.Precision.HIGHEST)
        / divisor[None, None]
    )
    return jnp.einsum("lk,pmkn->pmln", from_modes, modal, precision=lax.Precision.HIGHEST).astype(
        jnp.bfloat16
    )


def local(ensemble, counts, mixing, weights, legendre, to_modes, from_modes, mode_rates):
    traj_count = lax.axis_size("traj")
    lat_count = lax.axis_size("lat")
    local_waves = legendre.shape[0]
    degree_count = legendre.shape[2]
    total_waves = local_waves * lat_count
    longitudes = ensemble.shape[3]
    columns = np.arange(2 * total_waves)
    within = columns % (2 * local_waves)
    wavenumber = columns // (2 * local_waves) * local_waves + within % local_waves
    component = within // local_waves
    forward, backward = fourier_tables(wavenumber, component, longitudes)
    lat_scale = weights / longitudes
    divisor = mode_divisor(mode_rates, degree_count)
    vmem = pl.BlockSpec(memory_space=pltpu.VMEM)
    smem = pl.BlockSpec(memory_space=pltpu.SMEM)

    def to_spectral(received):
        split_parts = received.reshape(received.shape[0], received.shape[1], 2, local_waves)
        return jnp.einsum(
            "ljpm,mjn->pmln", split_parts, legendre, preferred_element_type=jnp.float32
        )

    def to_implicit(coefficients):
        spectral = to_spectral(
            lax.all_to_all(coefficients, "lat", split_axis=2, concat_axis=1, tiled=True)
        )
        return implicit_solve(spectral, to_modes, from_modes, divisor)

    def to_band_grid(implicit):
        row_lanes = -(-level_count * row_count // 128) * 128
        blocks = jax.ShapeDtypeStruct((lat_count, 2 * local_waves, row_lanes), jnp.bfloat16)
        band_blocks = pl.pallas_call(
            band_kernel,
            out_shape=blocks,
            in_specs=[vmem, vmem],
            out_specs=vmem,
            scratch_shapes=[
                pltpu.VMEM((2 * local_waves, lat_count * row_count, level_count), jnp.float32)
            ],
            name="band_legendre",
        )(implicit, legendre)
        return pl.pallas_call(
            last_kernel,
            out_shape=jax.ShapeDtypeStruct((level_count, row_count, longitudes), jnp.float32),
            in_specs=[vmem, vmem],
            out_specs=vmem,
            name="last_fourier",
        )(lax.all_to_all(band_blocks, "lat", 0, 0, tiled=True), backward)

    level_count, row_count = ensemble.shape[1], ensemble.shape[2]
    quarters = traj_count // local_waves
    modes = level_count // quarters
    used = modes * row_count
    lanes = -(-(used + 1) // 128) * 128
    pairs = np.arange(2 * total_waves)
    pair_wave = pairs // 2 % lat_count * local_waves + pairs // (2 * lat_count)
    pair_forward, pair_backward = fourier_tables(pair_wave, pairs % 2, longitudes)
    traj_index = lax.axis_index("traj")
    own_table = lax.dynamic_index_in_dim(legendre, traj_index // quarters, 0, keepdims=False)
    own_divisor = lax.dynamic_slice_in_dim(divisor, traj_index % quarters * modes, modes, 0)
    own_inverse = (1.0 / own_divisor).T

    outgoing = pl.pallas_call(
        first_kernel,
        out_shape=jax.ShapeDtypeStruct(
            (local_waves, quarters, lat_count, 2, lanes), jnp.bfloat16
        ),
        in_specs=[smem, smem, vmem, vmem, vmem, vmem],
        out_specs=vmem,
        scratch_shapes=[pltpu.VMEM((level_count, row_count, longitudes), jnp.float32)],
        name="first_fourier",
    )(
        counts.astype(jnp.float32),
        weights,
        np.ascontiguousarray(pair_forward.T),
        mixing,
        to_modes.astype(jnp.bfloat16),
        ensemble[0],
    )
    everyone = ("traj", "lat")
    arrived = lax.all_to_all(
        outgoing.reshape(traj_count * lat_count, 2, lanes), everyone, 0, 0, tiled=True
    )
    band_parts = pl.pallas_call(
        wave_kernel,
        out_shape=jax.ShapeDtypeStruct((traj_count, lat_count, 2, lanes), jnp.bfloat16),
        in_specs=[vmem, vmem, vmem, vmem],
        out_specs=vmem,
        scratch_shapes=[
            pltpu.VMEM((modes, lat_count * row_count, 2 * traj_count), jnp.float32),
            pltpu.VMEM((lat_count, used, 2 * traj_count), jnp.float32),
        ],
        name="wave_solve",
    )(
        arrived.reshape(traj_count, lat_count, 2, lanes),
        own_table,
        own_table.T,
        own_inverse,
    )
    returned = lax.all_to_all(
        band_parts.reshape(traj_count * lat_count, 2, lanes), everyone, 0, 0, tiled=True
    )
    modal_grid = pl.pallas_call(
        gather_kernel,
        out_shape=jax.ShapeDtypeStruct((level_count * row_count, longitudes), jnp.bfloat16),
        in_specs=[vmem, vmem],
        out_specs=vmem,
        name="gather_fourier",
    )(returned.reshape(local_waves, quarters, lat_count, 2, lanes), pair_backward)
    state_grid = mix_levels(from_modes, modal_grid.reshape(level_count, row_count, longitudes))
    state_grid = to_band_grid(to_implicit(grid_section(state_grid, mixing, lat_scale, forward)))
    return state_grid[None]


def solution(mesh):
    placed = (
        P("traj", None, "lat", None),
        P("traj"),
        P(),
        P("lat"),
        P("lat", None, None),
        P(),
        P(),
        P(),
    )
    return jax.shard_map(
        local, mesh=mesh, in_specs=placed, out_specs=P("traj", None, "lat", None), check_vma=False
    )
```

```python
import math

import jax
import jax.numpy as jnp
import numpy as np
from jax import lax
from jax.experimental import pallas as pl
from jax.experimental.pallas import tpu as pltpu
from jax.sharding import PartitionSpec as P

time_step = 0.3
cubic_rate = 0.1


def fourier_tables(wavenumber, component, longitudes):
    positions = np.arange(longitudes)
    product_index = positions[:, None] * wavenumber[None, :] % longitudes
    angles = 2.0 * math.pi / longitudes * product_index
    signed = np.where(component[None, :] == 0, np.cos(angles), -np.sin(angles))
    factor = np.where(wavenumber == 0, 1.0, 2.0)
    rounded = jnp.bfloat16
    return signed.astype(rounded), (factor[None, :] * signed).T.astype(rounded)


def mode_divisor(mode_rates, degree_count):
    degrees = jnp.arange(degree_count, dtype=jnp.float32)
    degree_ratio = degrees * (degrees + 1.0) / (degree_count * (degree_count + 1.0))
    return 1.0 + mode_rates[:, None] * degree_ratio[None, :]


def grid_tendency(state_grid, mixing):
    level_count, row_count, col_count = state_grid.shape
    rounded = state_grid.astype(jnp.bfloat16)
    mixing_term = jnp.dot(
        mixing,
        rounded.reshape(level_count, row_count * col_count),
        preferred_element_type=jnp.float32,
    ).reshape(level_count, row_count, col_count)
    tendency = state_grid + time_step * (
        mixing_term - cubic_rate * state_grid * state_grid * state_grid
    )
    return tendency.astype(jnp.bfloat16)


def mix_levels(matrix, grid):
    level_count, row_count, col_count = grid.shape
    flat = grid.reshape(level_count, row_count * col_count)
    mixed = jnp.dot(matrix.astype(jnp.bfloat16), flat, preferred_element_type=jnp.float32)
    return mixed.reshape(grid.shape)


def grid_section(state_grid, mixing, lat_scale, forward):
    level_count, row_count, col_count = state_grid.shape
    grid_rounded = grid_tendency(state_grid, mixing).reshape(level_count * row_count, col_count)
    fourier_sums = jnp.dot(grid_rounded, forward, preferred_element_type=jnp.float32)
    fourier_sums = fourier_sums.reshape(level_count, row_count, forward.shape[1])
    return (fourier_sums * lat_scale[None, :, None]).astype(jnp.bfloat16)


def contract(left, right, left_dim, right_dim):
    return lax.dot_general(
        left, right, (((left_dim,), (right_dim,)), ((), ())), preferred_element_type=jnp.float32
    )


def block_mask(rows, cols, test):
    row = lax.broadcasted_iota(jnp.int32, (rows, cols), 0)
    col = lax.broadcasted_iota(jnp.int32, (rows, cols), 1)
    return test(row, col)


def first_kernel(
    count_ref, weight_ref, table_ref, mixing_ref, to_ref, grid_ref, out_ref, modal_ref
):
    level_count, groups, _, longitudes = grid_ref.shape
    row_count = groups * 8
    wave_count, quarters, lat_count, _, lanes = out_ref.shape
    modes = level_count // quarters
    used = modes * row_count
    mixing, to_modes = mixing_ref[...], to_ref[...].astype(jnp.bfloat16)

    def advance(step, carry):
        for inner in range(8):
            row = step * 8 + inner
            state = grid_ref[:, step, inner, :]
            mixed = contract(mixing, state.astype(jnp.bfloat16), 1, 0)
            tendency = state + time_step * (mixed - cubic_rate * state * state * state)
            modal = contract(to_modes, tendency.astype(jnp.bfloat16), 1, 0)
            modal_ref[:, step, inner, :] = modal * (weight_ref[row] * (1.0 / longitudes))
        return carry

    lax.fori_loop(0, row_count // 8, advance, 0)
    table = table_ref[...]
    lane = lax.broadcasted_iota(jnp.int32, table.shape[:1] + (lanes,), 1)
    spare = jnp.zeros((lanes - used, longitudes), jnp.bfloat16)
    for quarter in range(quarters):
        block = modal_ref[quarter * modes : (quarter + 1) * modes]
        block = block.reshape(used, longitudes).astype(jnp.bfloat16)
        sums = contract(table, jnp.concatenate([block, spare], axis=0), 1, 1)
        sums = jnp.where(lane < used, sums, count_ref[0]).astype(jnp.bfloat16)
        out_ref[:, quarter] = sums.reshape(wave_count, lat_count, 2, lanes)


def selection(count_row, size):
    surplus = jnp.maximum(count_row - 1.0, 0.0).astype(jnp.bfloat16)
    dead = jnp.where(count_row == 0.0, 1.0, 0.0).astype(jnp.bfloat16)
    dead_all = jnp.broadcast_to(dead[0:1], (size, size))
    surplus_all = jnp.broadcast_to(surplus[0:1], (size, size))

    def ones_where(test):
        return jnp.where(block_mask(size, size, test), 1.0, 0.0).astype(jnp.bfloat16)

    upto = ones_where(lambda r, c: (r // 2 <= c // 2) & (r % 2 == 0))
    before = ones_where(lambda r, c: (c // 2 < r // 2) & (c % 2 == 0))
    same = ones_where(lambda r, c: r == c)
    surplus_end = contract(surplus_all, upto, 1, 0)
    killed_rank = contract(before, dead_all, 1, 1)
    killed = contract(same, dead_all, 1, 1)
    even = block_mask(size, size, lambda r, c: c % 2 == 0)
    pulled = jnp.sum(
        jnp.where(even & (surplus_end <= killed_rank), 1.0, 0.0), axis=1, keepdims=True
    )
    member = lax.broadcasted_iota(jnp.int32, (size, size), 0) // 2
    source = jnp.where(killed > 0.5, jnp.broadcast_to(pulled, (size, size)), member.astype(jnp.float32))
    picked = lax.broadcasted_iota(jnp.int32, (size, size), 1) // 2
    parity = block_mask(size, size, lambda r, c: r % 2 == c % 2)
    return jnp.where(parity & (picked.astype(jnp.float32) == source), 1.0, 0.0).astype(jnp.bfloat16)


def wave_kernel(parts_ref, table_ref, turned_ref, inverse_ref, out_ref, wave_ref, band_ref):
    members, lat_count, _, lanes = parts_ref.shape
    size = 2 * members
    modes, lat_rows, _ = wave_ref.shape
    rows = lat_rows // lat_count
    used = modes * rows
    unit = jnp.where(block_mask(used + 8, lanes, lambda r, c: r == c), 1.0, 0.0).astype(jnp.bfloat16)
    pick = None
    for lat in range(lat_count):
        turned = contract(unit, parts_ref[:, lat].reshape(size, lanes), 1, 1)
        if lat == 0:
            pick = selection(turned[used : used + 8], size)
        for mode in range(modes):
            wave_ref[mode, lat * rows : (lat + 1) * rows, :] = turned[mode * rows : (mode + 1) * rows]
    table = table_ref[...]
    turned_table = turned_ref[...]
    for mode in range(modes):
        spectral = contract(turned_table, wave_ref[mode].astype(jnp.bfloat16), 1, 0)
        modal = (spectral * inverse_ref[:, mode : mode + 1]).astype(jnp.bfloat16)
        band = contract(table, modal, 1, 0)
        for lat in range(lat_count):
            band_ref[lat, mode * rows : (mode + 1) * rows, :] = band[lat * rows : (lat + 1) * rows]
    spare = jnp.zeros((lanes - used, band_ref.shape[2]), jnp.bfloat16)
    for lat in range(lat_count):
        band = jnp.concatenate([band_ref[lat].astype(jnp.bfloat16), spare], axis=0)
        chosen = contract(pick, band, 1, 1).astype(jnp.bfloat16)
        out_ref[:, lat] = chosen.reshape(members, 2, lanes)


def band_kernel(implicit_ref, legendre_ref, out_ref, band_ref):
    lat_count, columns, lanes = out_ref.shape
    _, _, rows, level_count = band_ref.shape
    waves = legendre_ref.shape[0]
    for column in range(columns):
        own = implicit_ref[column // waves, column % waves]
        band = contract(legendre_ref[column % waves], own, 1, 1)
        band_ref[column] = band.reshape(lat_count, rows, level_count)
    used = rows * level_count

    def write(lat, carry):
        for row in range(rows):
            piece = band_ref[:, lat, row, :].astype(jnp.bfloat16)
            out_ref[lat, :, row * level_count : (row + 1) * level_count] = piece
        out_ref[lat, :, used:] = jnp.zeros((columns, lanes - used), jnp.bfloat16)
        return carry

    lax.fori_loop(0, lat_count, write, 0)


def last_kernel(table_ref, *refs):
    parts_refs, out_ref = refs[:-1], refs[-1]
    level_count, row_count, _ = out_ref.shape
    size = table_ref.shape[0] // len(parts_refs)
    parts = jnp.concatenate(
        [ref[...].reshape(size, ref.shape[2]) for ref in parts_refs], axis=0
    )
    sums = contract(parts, table_ref[...], 0, 0)
    for row in range(row_count):
        out_ref[:, row, :] = sums[row * level_count : (row + 1) * level_count]


def gather_kernel(parts_ref, table_ref, out_ref):
    _, quarters, _, _, lanes = parts_ref.shape
    used = out_ref.shape[0] // quarters
    for quarter in range(quarters):
        sums = contract(
            parts_ref[:, quarter].reshape(table_ref.shape[0], lanes), table_ref[...], 0, 0
        )
        out_ref[quarter * used : (quarter + 1) * used, :] = sums[:used].astype(jnp.bfloat16)


def implicit_solve(spectral, to_modes, from_modes, divisor):
    modal = (
        jnp.einsum("kl,pmln->pmkn", to_modes, spectral, precision=lax.Precision.HIGHEST)
        / divisor[None, None]
    )
    return jnp.einsum("lk,pmkn->pmln", from_modes, modal, precision=lax.Precision.HIGHEST).astype(
        jnp.bfloat16
    )


def local(ensemble, counts, mixing, weights, legendre, to_modes, from_modes, mode_rates):
    traj_count = lax.axis_size("traj")
    lat_count = lax.axis_size("lat")
    local_waves = legendre.shape[0]
    degree_count = legendre.shape[2]
    total_waves = local_waves * lat_count
    longitudes = ensemble.shape[3]
    halves = 2
    half_waves = local_waves // halves
    columns = np.arange(2 * total_waves)
    half = columns // (2 * total_waves // halves)
    within = columns % (2 * half_waves)
    owner = columns // (2 * half_waves) % lat_count
    wavenumber = owner * local_waves + half * half_waves + within % half_waves
    forward, backward = fourier_tables(wavenumber, within // half_waves, longitudes)
    lat_scale = weights / longitudes
    divisor = mode_divisor(mode_rates, degree_count)
    vmem = pl.BlockSpec(memory_space=pltpu.VMEM)
    smem = pl.BlockSpec(memory_space=pltpu.SMEM)

    def to_implicit(coefficients, table):
        received = lax.all_to_all(coefficients, "lat", split_axis=2, concat_axis=1, tiled=True)
        split_parts = received.reshape(received.shape[0], received.shape[1], 2, half_waves)
        spectral = jnp.einsum(
            "ljpm,mjn->pmln", split_parts, table, preferred_element_type=jnp.float32
        )
        return implicit_solve(spectral, to_modes, from_modes, divisor)

    def to_band(implicit, table):
        row_lanes = -(-level_count * row_count // 128) * 128
        band_blocks = pl.pallas_call(
            band_kernel,
            out_shape=jax.ShapeDtypeStruct((lat_count, 2 * half_waves, row_lanes), jnp.bfloat16),
            in_specs=[vmem, vmem],
            out_specs=vmem,
            scratch_shapes=[
                pltpu.VMEM((2 * half_waves, lat_count, row_count, level_count), jnp.float32)
            ],
            name="band_legendre",
        )(implicit, table)
        return lax.all_to_all(band_blocks, "lat", 0, 0, tiled=True)

    level_count, row_count = ensemble.shape[1], ensemble.shape[2]
    quarters = traj_count // local_waves
    modes = level_count // quarters
    used = modes * row_count
    lanes = -(-(used + 1) // 128) * 128
    pairs = np.arange(2 * total_waves)
    pair_wave = pairs // 2 % lat_count * local_waves + pairs // (2 * lat_count)
    pair_forward, pair_backward = fourier_tables(pair_wave, pairs % 2, longitudes)
    traj_index = lax.axis_index("traj")
    own_table = lax.dynamic_index_in_dim(legendre, traj_index // quarters, 0, keepdims=False)
    own_divisor = lax.dynamic_slice_in_dim(divisor, traj_index % quarters * modes, modes, 0)
    own_inverse = (1.0 / own_divisor).T

    outgoing = pl.pallas_call(
        first_kernel,
        out_shape=jax.ShapeDtypeStruct(
            (local_waves, quarters, lat_count, 2, lanes), jnp.bfloat16
        ),
        in_specs=[smem, smem, vmem, vmem, vmem, vmem],
        out_specs=vmem,
        scratch_shapes=[pltpu.VMEM((level_count, row_count // 8, 8, longitudes), jnp.float32)],
        name="first_fourier",
    )(
        counts.astype(jnp.float32),
        weights,
        np.ascontiguousarray(pair_forward.T),
        mixing,
        to_modes,
        ensemble.reshape(level_count, row_count // 8, 8, longitudes),
    )
    everyone = ("traj", "lat")
    arrived = lax.all_to_all(
        outgoing.reshape(traj_count * lat_count, 2, lanes), everyone, 0, 0, tiled=True
    )
    band_parts = pl.pallas_call(
        wave_kernel,
        out_shape=jax.ShapeDtypeStruct((traj_count, lat_count, 2, lanes), jnp.bfloat16),
        in_specs=[vmem, vmem, vmem, vmem],
        out_specs=vmem,
        scratch_shapes=[
            pltpu.VMEM((modes, lat_count * row_count, 2 * traj_count), jnp.float32),
            pltpu.VMEM((lat_count, used, 2 * traj_count), jnp.float32),
        ],
        name="wave_solve",
    )(
        arrived.reshape(traj_count, lat_count, 2, lanes),
        own_table,
        own_table.T,
        own_inverse,
    )
    returned = lax.all_to_all(
        band_parts.reshape(traj_count * lat_count, 2, lanes), everyone, 0, 0, tiled=True
    )
    modal_grid = pl.pallas_call(
        gather_kernel,
        out_shape=jax.ShapeDtypeStruct((level_count * row_count, longitudes), jnp.bfloat16),
        in_specs=[vmem, vmem],
        out_specs=vmem,
        name="gather_fourier",
    )(returned.reshape(local_waves, quarters, lat_count, 2, lanes), pair_backward)
    state_grid = mix_levels(from_modes, modal_grid.reshape(level_count, row_count, longitudes))
    coefficients = grid_section(state_grid, mixing, lat_scale, forward)
    share = 2 * total_waves // halves
    tables = [legendre[at * half_waves : (at + 1) * half_waves] for at in range(halves)]
    implicit = [
        to_implicit(coefficients[:, :, at * share : (at + 1) * share], tables[at])
        for at in range(halves)
    ]
    bands = [to_band(implicit[at], tables[at]) for at in range(halves)]
    state_grid = pl.pallas_call(
        last_kernel,
        out_shape=jax.ShapeDtypeStruct((level_count, row_count, longitudes), jnp.float32),
        in_specs=[vmem] * (halves + 1),
        out_specs=vmem,
        name="last_fourier",
    )(backward, *bands)
    return state_grid[None]


def solution(mesh):
    placed = (
        P("traj", None, "lat", None),
        P("traj"),
        P(),
        P("lat"),
        P("lat", None, None),
        P(),
        P(),
        P(),
    )
    return jax.shard_map(
        local, mesh=mesh, in_specs=placed, out_specs=P("traj", None, "lat", None), check_vma=False
    )
```

```python
import math

import jax
import jax.numpy as jnp
import numpy as np
from jax import lax
from jax.experimental import pallas as pl
from jax.experimental.pallas import tpu as pltpu
from jax.sharding import PartitionSpec as P

time_step = 0.3
cubic_rate = 0.1


def fourier_tables(wavenumber, component, longitudes):
    positions = np.arange(longitudes)
    product_index = positions[:, None] * wavenumber[None, :] % longitudes
    angles = 2.0 * math.pi / longitudes * product_index
    signed = np.where(component[None, :] == 0, np.cos(angles), -np.sin(angles))
    factor = np.where(wavenumber == 0, 1.0, 2.0)
    rounded = jnp.bfloat16
    return signed.astype(rounded), (factor[None, :] * signed).T.astype(rounded)


def mode_divisor(mode_rates, degree_count):
    degrees = jnp.arange(degree_count, dtype=jnp.float32)
    degree_ratio = degrees * (degrees + 1.0) / (degree_count * (degree_count + 1.0))
    return 1.0 + mode_rates[:, None] * degree_ratio[None, :]


def grid_tendency(state_grid, mixing):
    level_count, row_count, col_count = state_grid.shape
    rounded = state_grid.astype(jnp.bfloat16)
    mixing_term = jnp.dot(
        mixing,
        rounded.reshape(level_count, row_count * col_count),
        preferred_element_type=jnp.float32,
    ).reshape(level_count, row_count, col_count)
    tendency = state_grid + time_step * (
        mixing_term - cubic_rate * state_grid * state_grid * state_grid
    )
    return tendency.astype(jnp.bfloat16)


def mix_levels(matrix, grid):
    level_count, row_count, col_count = grid.shape
    flat = grid.reshape(level_count, row_count * col_count)
    mixed = jnp.dot(matrix.astype(jnp.bfloat16), flat, preferred_element_type=jnp.float32)
    return mixed.reshape(grid.shape)


def grid_section(state_grid, mixing, lat_scale, forward):
    level_count, row_count, col_count = state_grid.shape
    grid_rounded = grid_tendency(state_grid, mixing).reshape(level_count * row_count, col_count)
    fourier_sums = jnp.dot(grid_rounded, forward, preferred_element_type=jnp.float32)
    fourier_sums = fourier_sums.reshape(level_count, row_count, forward.shape[1])
    return (fourier_sums * lat_scale[None, :, None]).astype(jnp.bfloat16)


def contract(left, right, left_dim, right_dim):
    return lax.dot_general(
        left, right, (((left_dim,), (right_dim,)), ((), ())), preferred_element_type=jnp.float32
    )


def block_mask(rows, cols, test):
    row = lax.broadcasted_iota(jnp.int32, (rows, cols), 0)
    col = lax.broadcasted_iota(jnp.int32, (rows, cols), 1)
    return test(row, col)


def first_kernel(
    count_ref, weight_ref, table_ref, mixing_ref, to_ref, grid_ref, out_ref, modal_ref
):
    level_count, groups, _, longitudes = grid_ref.shape
    row_count = groups * 8
    wave_count, quarters, lat_count, _, lanes = out_ref.shape
    modes = level_count // quarters
    used = modes * row_count
    mixing, to_modes = mixing_ref[...], to_ref[...].astype(jnp.bfloat16)

    def advance(step, carry):
        for inner in range(8):
            row = step * 8 + inner
            state = grid_ref[:, step, inner, :]
            mixed = contract(mixing, state.astype(jnp.bfloat16), 1, 0)
            tendency = state + time_step * (mixed - cubic_rate * state * state * state)
            modal = contract(to_modes, tendency.astype(jnp.bfloat16), 1, 0)
            modal_ref[:, step, inner, :] = modal * (weight_ref[row] * (1.0 / longitudes))
        return carry

    lax.fori_loop(0, row_count // 8, advance, 0)
    table = table_ref[...]
    lane = lax.broadcasted_iota(jnp.int32, table.shape[:1] + (lanes,), 1)
    spare = jnp.zeros((lanes - used, longitudes), jnp.bfloat16)
    for quarter in range(quarters):
        block = modal_ref[quarter * modes : (quarter + 1) * modes]
        block = block.reshape(used, longitudes).astype(jnp.bfloat16)
        sums = contract(table, jnp.concatenate([block, spare], axis=0), 1, 1)
        sums = jnp.where(lane < used, sums, count_ref[0]).astype(jnp.bfloat16)
        out_ref[:, quarter] = sums.reshape(wave_count, lat_count, 2, lanes)


def selection(count_row, size):
    surplus = jnp.maximum(count_row - 1.0, 0.0).astype(jnp.bfloat16)
    dead = jnp.where(count_row == 0.0, 1.0, 0.0).astype(jnp.bfloat16)
    dead_all = jnp.broadcast_to(dead[0:1], (size, size))
    surplus_all = jnp.broadcast_to(surplus[0:1], (size, size))

    def ones_where(test):
        return jnp.where(block_mask(size, size, test), 1.0, 0.0).astype(jnp.bfloat16)

    upto = ones_where(lambda r, c: (r // 2 <= c // 2) & (r % 2 == 0))
    before = ones_where(lambda r, c: (c // 2 < r // 2) & (c % 2 == 0))
    same = ones_where(lambda r, c: r == c)
    surplus_end = contract(surplus_all, upto, 1, 0)
    killed_rank = contract(before, dead_all, 1, 1)
    killed = contract(same, dead_all, 1, 1)
    even = block_mask(size, size, lambda r, c: c % 2 == 0)
    pulled = jnp.sum(
        jnp.where(even & (surplus_end <= killed_rank), 1.0, 0.0), axis=1, keepdims=True
    )
    member = lax.broadcasted_iota(jnp.int32, (size, size), 0) // 2
    source = jnp.where(killed > 0.5, jnp.broadcast_to(pulled, (size, size)), member.astype(jnp.float32))
    picked = lax.broadcasted_iota(jnp.int32, (size, size), 1) // 2
    parity = block_mask(size, size, lambda r, c: r % 2 == c % 2)
    return jnp.where(parity & (picked.astype(jnp.float32) == source), 1.0, 0.0).astype(jnp.bfloat16)


def wave_kernel(parts_ref, table_ref, turned_ref, inverse_ref, out_ref, wave_ref, band_ref):
    members, lat_count, _, lanes = parts_ref.shape
    size = 2 * members
    modes, lat_rows, _ = wave_ref.shape
    rows = lat_rows // lat_count
    used = modes * rows
    unit = jnp.where(block_mask(used + 8, lanes, lambda r, c: r == c), 1.0, 0.0).astype(jnp.bfloat16)
    pick = None
    for lat in range(lat_count):
        turned = contract(unit, parts_ref[:, lat].reshape(size, lanes), 1, 1)
        if lat == 0:
            pick = selection(turned[used : used + 8], size)
        for mode in range(modes):
            wave_ref[mode, lat * rows : (lat + 1) * rows, :] = turned[mode * rows : (mode + 1) * rows]
    table = table_ref[...]
    turned_table = turned_ref[...]
    for mode in range(modes):
        spectral = contract(turned_table, wave_ref[mode].astype(jnp.bfloat16), 1, 0)
        modal = (spectral * inverse_ref[:, mode : mode + 1]).astype(jnp.bfloat16)
        band = contract(table, modal, 1, 0)
        for lat in range(lat_count):
            band_ref[lat, mode * rows : (mode + 1) * rows, :] = band[lat * rows : (lat + 1) * rows]
    spare = jnp.zeros((lanes - used, band_ref.shape[2]), jnp.bfloat16)
    for lat in range(lat_count):
        band = jnp.concatenate([band_ref[lat].astype(jnp.bfloat16), spare], axis=0)
        chosen = contract(pick, band, 1, 1).astype(jnp.bfloat16)
        out_ref[:, lat] = chosen.reshape(members, 2, lanes)


def band_kernel(implicit_ref, legendre_ref, out_ref, band_ref):
    lat_count, columns, lanes = out_ref.shape
    _, all_rows, level_count = band_ref.shape
    rows = all_rows // lat_count
    waves = legendre_ref.shape[0]
    for column in range(columns):
        own = implicit_ref[column // waves, column % waves]
        band_ref[column] = contract(legendre_ref[column % waves], own, 1, 1)
    for lat in range(lat_count):
        for row in range(rows):
            piece = band_ref[:, lat * rows + row, :].astype(jnp.bfloat16)
            out_ref[lat, :, row * level_count : (row + 1) * level_count] = piece
    used = rows * level_count
    out_ref[:, :, used:] = jnp.zeros((lat_count, columns, lanes - used), jnp.bfloat16)


def last_kernel(parts_ref, table_ref, out_ref):
    level_count, row_count, _ = out_ref.shape
    parts = parts_ref[...].reshape(table_ref.shape[0], parts_ref.shape[2])
    sums = contract(parts, table_ref[...], 0, 0)
    for row in range(row_count):
        out_ref[:, row, :] = sums[row * level_count : (row + 1) * level_count]


def gather_kernel(parts_ref, table_ref, out_ref):
    _, quarters, _, _, lanes = parts_ref.shape
    used = out_ref.shape[0] // quarters
    for quarter in range(quarters):
        sums = contract(
            parts_ref[:, quarter].reshape(table_ref.shape[0], lanes), table_ref[...], 0, 0
        )
        out_ref[quarter * used : (quarter + 1) * used, :] = sums[:used].astype(jnp.bfloat16)


def implicit_solve(spectral, to_modes, from_modes, divisor):
    modal = (
        jnp.einsum("kl,pmln->pmkn", to_modes, spectral, precision=lax.Precision.HIGH)
        / divisor[None, None]
    )
    return jnp.einsum("lk,pmkn->pmln", from_modes, modal, precision=lax.Precision.HIGH).astype(
        jnp.bfloat16
    )


def local(ensemble, counts, mixing, weights, legendre, to_modes, from_modes, mode_rates):
    traj_count = lax.axis_size("traj")
    lat_count = lax.axis_size("lat")
    local_waves = legendre.shape[0]
    degree_count = legendre.shape[2]
    total_waves = local_waves * lat_count
    longitudes = ensemble.shape[3]
    columns = np.arange(2 * total_waves)
    within = columns % (2 * local_waves)
    wavenumber = columns // (2 * local_waves) * local_waves + within % local_waves
    component = within // local_waves
    forward, backward = fourier_tables(wavenumber, component, longitudes)
    lat_scale = weights / longitudes
    divisor = mode_divisor(mode_rates, degree_count)
    vmem = pl.BlockSpec(memory_space=pltpu.VMEM)
    smem = pl.BlockSpec(memory_space=pltpu.SMEM)

    def to_spectral(received):
        split_parts = received.reshape(received.shape[0], received.shape[1], 2, local_waves)
        return jnp.einsum(
            "ljpm,mjn->pmln", split_parts, legendre, preferred_element_type=jnp.float32
        )

    def to_implicit(coefficients):
        spectral = to_spectral(
            lax.all_to_all(coefficients, "lat", split_axis=2, concat_axis=1, tiled=True)
        )
        return implicit_solve(spectral, to_modes, from_modes, divisor)

    def to_band_grid(implicit):
        row_lanes = -(-level_count * row_count // 128) * 128
        blocks = jax.ShapeDtypeStruct((lat_count, 2 * local_waves, row_lanes), jnp.bfloat16)
        band_blocks = pl.pallas_call(
            band_kernel,
            out_shape=blocks,
            in_specs=[vmem, vmem],
            out_specs=vmem,
            scratch_shapes=[
                pltpu.VMEM((2 * local_waves, lat_count * row_count, level_count), jnp.float32)
            ],
            name="band_legendre",
        )(implicit, legendre)
        return pl.pallas_call(
            last_kernel,
            out_shape=jax.ShapeDtypeStruct((level_count, row_count, longitudes), jnp.float32),
            in_specs=[vmem, vmem],
            out_specs=vmem,
            name="last_fourier",
        )(lax.all_to_all(band_blocks, "lat", 0, 0, tiled=True), backward)

    level_count, row_count = ensemble.shape[1], ensemble.shape[2]
    quarters = traj_count // local_waves
    modes = level_count // quarters
    used = modes * row_count
    lanes = -(-(used + 1) // 128) * 128
    pairs = np.arange(2 * total_waves)
    pair_wave = pairs // 2 % lat_count * local_waves + pairs // (2 * lat_count)
    pair_forward, pair_backward = fourier_tables(pair_wave, pairs % 2, longitudes)
    traj_index = lax.axis_index("traj")
    own_table = lax.dynamic_index_in_dim(legendre, traj_index // quarters, 0, keepdims=False)
    own_divisor = lax.dynamic_slice_in_dim(divisor, traj_index % quarters * modes, modes, 0)
    own_inverse = (1.0 / own_divisor).T

    outgoing = pl.pallas_call(
        first_kernel,
        out_shape=jax.ShapeDtypeStruct(
            (local_waves, quarters, lat_count, 2, lanes), jnp.bfloat16
        ),
        in_specs=[smem, smem, vmem, vmem, vmem, vmem],
        out_specs=vmem,
        scratch_shapes=[pltpu.VMEM((level_count, row_count // 8, 8, longitudes), jnp.float32)],
        name="first_fourier",
    )(
        counts.astype(jnp.float32),
        weights,
        np.ascontiguousarray(pair_forward.T),
        mixing,
        to_modes,
        ensemble.reshape(level_count, row_count // 8, 8, longitudes),
    )
    everyone = ("traj", "lat")
    arrived = lax.all_to_all(
        outgoing.reshape(traj_count * lat_count, 2, lanes), everyone, 0, 0, tiled=True
    )
    band_parts = pl.pallas_call(
        wave_kernel,
        out_shape=jax.ShapeDtypeStruct((traj_count, lat_count, 2, lanes), jnp.bfloat16),
        in_specs=[vmem, vmem, vmem, vmem],
        out_specs=vmem,
        scratch_shapes=[
            pltpu.VMEM((modes, lat_count * row_count, 2 * traj_count), jnp.float32),
            pltpu.VMEM((lat_count, used, 2 * traj_count), jnp.float32),
        ],
        name="wave_solve",
    )(
        arrived.reshape(traj_count, lat_count, 2, lanes),
        own_table,
        own_table.T,
        own_inverse,
    )
    returned = lax.all_to_all(
        band_parts.reshape(traj_count * lat_count, 2, lanes), everyone, 0, 0, tiled=True
    )
    modal_grid = pl.pallas_call(
        gather_kernel,
        out_shape=jax.ShapeDtypeStruct((level_count * row_count, longitudes), jnp.bfloat16),
        in_specs=[vmem, vmem],
        out_specs=vmem,
        name="gather_fourier",
    )(returned.reshape(local_waves, quarters, lat_count, 2, lanes), pair_backward)
    state_grid = mix_levels(from_modes, modal_grid.reshape(level_count, row_count, longitudes))
    state_grid = to_band_grid(to_implicit(grid_section(state_grid, mixing, lat_scale, forward)))
    return state_grid[None]


def solution(mesh):
    placed = (
        P("traj", None, "lat", None),
        P("traj"),
        P(),
        P("lat"),
        P("lat", None, None),
        P(),
        P(),
        P(),
    )
    return jax.shard_map(
        local, mesh=mesh, in_specs=placed, out_specs=P("traj", None, "lat", None), check_vma=False
    )
```
